32 devices in a mesh: expert: 16 (over z, y, core), replica: 2 (over x).
Axes of the slice: x: 2, y: 2, z: 4, core: 2. Of those that a mesh axis runs over, the one named last changes fastest.
Arguments:
- tokens: bfloat16 [768, 7168], P('expert', 'replica'), may hold values from -18 to 18
- expert_ids: int32 [768, 8], P('expert'), may hold values from 0 to 15, all different within a row; in each aligned block of 48 rows (0 to 47, 48 to 95, ...) at most 48 rows name the same one
- route_weights: bfloat16 [768, 8], P('expert'), may hold values from 0.1 to 1.5
- gate_weight: bfloat16 [16, 7168, 1024], P('expert', 'replica'), may hold values from -0.0625 to 0.0625
- up_weight: bfloat16 [16, 7168, 1024], P('expert', 'replica'), may hold values from -0.0625 to 0.0625
- down_weight: bfloat16 [16, 1024, 7168], P('expert', None, 'replica'), may hold values from -0.1875 to 0.1875
- bin_edges: float32 [16], replicated, may hold values from 0 to 20, as said below
Outputs:
- mixed: bfloat16 [768, 7168], P('expert', 'replica')
- expert_load: float32 [16], P('expert')
The draws below stay inside these ranges and needn't reach their ends.
Inputs may be any that keep to these rules, and one draw needn't show every extreme that they name: `expert_ids`: each row names 8 different experts; within the 48 rows of one index of expert no expert is named by more than 48 rows, a bound that some block reaches. `bin_edges`: strictly increasing and positive; the last edge is 20, above every token entry's magnitude.
All inputs are finite; a program needn't handle non-finite values.
Results may differ from the reference program's by a relative error of at most 0.019.
Values may be sent and summed in bfloat16 or wider, within the bound.
A program may use at most 128 MiB of HBM per device.

```python
import math
import jax
import jax.numpy as jnp
import numpy as np
from jax import lax

D = 7168
FF = 1024
TOP = 8
BINS = 16
FINE = 8
TOK_DEV = 48
EXPERTS = 16
CAP = 48
TOKENS = 768
N_EXPERT = 16
N_REPLICA = 2


def draw_tokens(key, part):
    first = jax.random.fold_in(key, 11)
    second = jax.random.fold_in(key, 12)
    third = jax.random.fold_in(key, 13)
    channel_spread = jnp.exp(jax.random.uniform(second, (D,), jnp.float32, jnp.log(0.25), jnp.log(2.5)))
    row_spread = jnp.exp(jax.random.uniform(third, (TOKENS,), jnp.float32, jnp.log(0.5), jnp.log(1.2)))
    base = jnp.clip(jax.random.normal(first, (TOKENS, D), jnp.float32), -6.0, 6.0)
    return (base * channel_spread[None, :] * row_spread[:, None]).astype(jnp.bfloat16)


def draw_route_weights(key, part):
    blocks_all = TOKENS // TOK_DEV
    block_place = (jnp.arange(TOKENS, dtype=jnp.int32) // TOK_DEV).astype(jnp.float32)
    fraction = block_place / max(blocks_all - 1, 1)
    base = jax.random.uniform(jax.random.fold_in(key, 31), (TOKENS, TOP), jnp.float32, 0.1, 0.5)
    rising = 1.0 + 2.0 * fraction
    return (base * rising[:, None]).astype(jnp.bfloat16)


def draw_bin_edges(key, part):
    widths = jnp.exp(jax.random.uniform(jax.random.fold_in(key, 21), (BINS,), jnp.float32, jnp.log(0.5), jnp.log(2.0)))
    edges = 20.0 * jnp.cumsum(widths) / jnp.sum(widths)
    return edges.at[BINS - 1].set(20.0)


def shard_levels(rng, extent, shards, low, largest):
    gain, own = 1.0, jax.random.fold_in(rng, 6)
    for dim, shards_of in shards:
        steps = jnp.exp(jax.random.uniform(jax.random.fold_in(own, dim), (shards_of,), jnp.float32, low / len(shards), largest / len(shards)))
        gain = gain * jnp.repeat(steps, extent[dim] // shards_of).reshape([-1 if axis == dim else 1 for axis in range(len(extent))])
    return gain


def deal_out(stream_key, own, number, rows, count, top, most, skew):
    order = jax.random.permutation(stream_key, count)
    crowded, common = load_shares(count, rows * top, most, skew, True), load_shares(count, rows * top, most, skew, False)
    places = jnp.arange(count)

    def named(sizes, rotation):
        used = int((sizes > 0).sum())
        fixed = max(1, used // 4)
        passed = fixed + (places - fixed + rotation * (used - fixed)) % max(1, count - fixed)
        return jnp.zeros((count,), jnp.int32).at[order[jnp.where(places < fixed, places, passed)]].set(jnp.asarray(sizes, jnp.int32))

    sizes = jnp.where(number % 4 == 0, named(crowded, number // 4), named(common, number - number // 4 - 1))
    mixed = jax.random.permutation(jax.random.fold_in(own, 3), count)
    donor, taker = mixed[0:count // 2 * 2:2], mixed[1:count // 2 * 2:2]
    margin = jnp.minimum(sizes[donor] - 1, most - sizes[taker]) // 2
    margin = jnp.where((donor == order[0]) | (taker == order[0]) | (sizes[taker] == 0), 0, jnp.maximum(margin, 0))
    passed = jax.random.randint(jax.random.fold_in(own, 4), (count // 2,), 0, 1 << 20) % (margin + 1)
    sizes = sizes.at[donor].add(-passed).at[taker].add(passed)
    labels = jnp.searchsorted(jnp.cumsum(sizes), jnp.arange(rows * top), side="right").astype(jnp.int32)
    grid = labels.reshape(top, rows).T
    grid = grid[jax.random.permutation(jax.random.fold_in(own, 1), rows)]
    rotation = jax.random.randint(jax.random.fold_in(own, 2), (rows, 1), 0, top)
    return jnp.take_along_axis(grid, (jnp.arange(top)[None, :] + rotation) % top, axis=1)


def load_shares(count, total, reach, slope, full):
    portions = [(1 << 20) // math.isqrt(grade ** slope) + 1 for grade in range(1, count + 1)]
    largest = reach if full else min(reach, max(-(-total // count), total * portions[0] // sum(portions)))
    least = 1 if total - largest >= count - 1 else 0
    holding, rest = [largest] + [least] * (count - 1), total - largest - least * (count - 1)
    while rest > 0:
        free = [i for i in range(1, count) if holding[i] < largest] or [i for i in range(1, count) if holding[i] < reach]
        pool, budget = sum([portions[i] for i in free]), rest
        for i in free:
            addition = min(reach - holding[i], max(1, budget * portions[i] // pool), rest)
            holding[i] = holding[i] + addition
            rest = rest - addition
    return np.array(holding)


def bell_draw(key, extent, scale, reach, shards=(), kind=jnp.bfloat16):
    array = scale * jax.random.normal(key, extent, jnp.float32)
    if shards:
        array = array * shard_levels(key, extent, shards, -0.22, 0.18)
    return jnp.clip(array, -reach, reach).astype(kind)


def setup_inputs(seed: int = 0) -> dict:
    key_list = jax.random.split(jax.random.key(seed), 8)
    tokens = draw_tokens(jax.random.fold_in(key_list[7], 71), 0)
    expert_ids_keys = jax.random.split(jax.random.fold_in(key_list[1], 1), TOKENS // TOK_DEV)
    expert_ids_turns = jax.random.permutation(jax.random.fold_in(key_list[1], 3), TOKENS // TOK_DEV)
    expert_ids = jax.vmap(lambda own, number: deal_out(jax.random.fold_in(key_list[1], 2), own, number, TOK_DEV, EXPERTS, TOP, CAP, 2))(expert_ids_keys, expert_ids_turns).reshape((TOKENS, TOP))
    route_weights = draw_route_weights(jax.random.fold_in(key_list[7], 71), 0)
    gate_weight = bell_draw(key_list[3], (EXPERTS, D, FF), D ** -0.5, 0.0625, ((0, 16), (1, 2)))
    up_weight = bell_draw(key_list[4], (EXPERTS, D, FF), D ** -0.5, 0.0625, ((0, 16), (1, 2)))
    down_weight = bell_draw(key_list[5], (EXPERTS, FF, D), FF ** -0.5, 0.1875, ((0, 16), (2, 2)))
    bin_edges = draw_bin_edges(jax.random.fold_in(key_list[7], 71), 0)
    return {"tokens": tokens, "expert_ids": expert_ids, "route_weights": route_weights, "gate_weight": gate_weight, "up_weight": up_weight, "down_weight": down_weight, "bin_edges": bin_edges}


clip_parts = 8


def above_counts(magnitude, levels):
    return lax.map(lambda level: jnp.sum((magnitude >= level).astype(jnp.int32), axis=0), levels)


def clip_scales(magnitude, edges, limit):
    coarse = above_counts(magnitude, edges)
    chosen = jnp.sum((coarse > limit).astype(jnp.int32), axis=0)
    places = jnp.arange(edges.shape[0], dtype=jnp.int32)
    upper = jnp.sum(jnp.where(places[:, None] == chosen[None, :], edges[:, None], jnp.zeros_like(edges)[:, None]), axis=0)
    lower = jnp.sum(jnp.where(places[:, None] == chosen[None, :] - 1, edges[:, None], jnp.zeros_like(edges)[:, None]), axis=0)
    fractions = jnp.arange(1, FINE + 1).astype(edges.dtype) / FINE
    levels = lower[None, :] + (upper - lower)[None, :] * fractions[:, None]
    levels = jnp.concatenate([levels[:-1], upper[None, :]], axis=0)
    refined = above_counts(magnitude, levels)
    picked = jnp.sum((refined > limit).astype(jnp.int32), axis=0)
    steps = jnp.arange(FINE, dtype=jnp.int32)
    return jnp.sum(jnp.where(steps[:, None] == picked[None, :], levels, jnp.zeros_like(levels)), axis=0)


def reference(tokens, expert_ids, route_weights, gate_weight, up_weight, down_weight, bin_edges):
    slots = N_EXPERT * CAP
    share = D // N_REPLICA
    flat_ids = expert_ids.reshape(-1)
    blocks = expert_ids.reshape(N_EXPERT, TOK_DEV * TOP)
    hits = (blocks[:, :, None] == jnp.arange(EXPERTS, dtype=jnp.int32)[None, None, :]).astype(jnp.int32)
    ranks = jnp.sum((jnp.cumsum(hits, axis=1) - hits) * hits, axis=2)
    sources = jnp.arange(N_EXPERT, dtype=jnp.int32)[:, None]
    position = (sources * CAP + ranks).reshape(-1).astype(jnp.int32)
    owner = (jnp.arange(TOKENS * TOP, dtype=jnp.int32) // TOP).astype(jnp.int32)
    weights = route_weights.reshape(-1).astype(jnp.float32)
    padded = jnp.concatenate([tokens, jnp.zeros((1, D), tokens.dtype)], axis=0)
    block_weights = weights.reshape(N_EXPERT, TOK_DEV * TOP)
    weight_sums = jnp.sum(hits.astype(jnp.float32) * block_weights[:, :, None], axis=(0, 1))
    expert_load = weight_sums * EXPERTS / (TOKENS * TOP)

    def one_expert(total, inputs):
        gate_w, up_w, down_w, number = inputs
        match = flat_ids == number
        target = jnp.where(match, position, slots).astype(jnp.int32)
        row_owner = jnp.full((slots,), TOKENS, jnp.int32).at[target].set(owner, mode="drop")
        row_weight = jnp.zeros((slots,), jnp.float32).at[target].set(weights, mode="drop")
        rows = padded[row_owner]
        limit = jnp.sum(match.astype(jnp.int32)) // clip_parts
        scale = clip_scales(jnp.abs(rows), bin_edges, limit)
        quantized = (jnp.clip(rows.astype(jnp.float32), -scale, scale) / scale).astype(jnp.bfloat16)
        gate_fold = (gate_w.astype(jnp.float32) * scale[:, None]).astype(jnp.bfloat16)
        up_fold = (up_w.astype(jnp.float32) * scale[:, None]).astype(jnp.bfloat16)
        gate = jnp.zeros((slots, FF), jnp.float32)
        up_sum = jnp.zeros((slots, FF), jnp.float32)
        for block in range(N_REPLICA):
            low = block * share
            piece = quantized[:, low:low + share].astype(jnp.float32)
            gate_part = jnp.dot(piece, gate_fold[low:low + share].astype(jnp.float32), precision=lax.Precision.HIGHEST)
            up_part = jnp.dot(piece, up_fold[low:low + share].astype(jnp.float32), precision=lax.Precision.HIGHEST)
            gate = gate + lax.optimization_barrier(gate_part.astype(jnp.bfloat16)).astype(jnp.float32)
            up_sum = up_sum + lax.optimization_barrier(up_part.astype(jnp.bfloat16)).astype(jnp.float32)
        hidden = (jax.nn.silu(gate) * up_sum).astype(jnp.bfloat16)
        result = jnp.dot(hidden.astype(jnp.float32), down_w.astype(jnp.float32), precision=lax.Precision.HIGHEST)
        result = lax.optimization_barrier(result.astype(jnp.bfloat16)).astype(jnp.float32)
        total = total.at[row_owner].add(row_weight[:, None] * result, mode="drop")
        return total, None

    numbers = jnp.arange(EXPERTS, dtype=jnp.int32)
    total, _ = lax.scan(one_expert, jnp.zeros((TOKENS, D), jnp.float32), (gate_weight, up_weight, down_weight, numbers))
    return total.astype(jnp.bfloat16), expert_load
```

```python
import functools

import jax
import jax.numpy as jnp
from jax import lax
from jax.experimental import pallas as pl
from jax.experimental.pallas import tpu as pltpu
from jax.sharding import PartitionSpec as P

FINE = 8
clip_parts = 8


def round_up(level):
    near = level.astype(jnp.bfloat16)
    wide = near.astype(jnp.float32)
    above = (wide * (1.0 + 0.75 * 2.0**-7)).astype(jnp.bfloat16)
    return jnp.where(wide < level, above.astype(jnp.float32), wide).astype(jnp.bfloat16)


def counts(magnitude_ref, level):
    rows, width = magnitude_ref.shape
    bound = jnp.broadcast_to(round_up(level), (16, width))
    one, zero = jnp.ones((16, width), jnp.bfloat16), jnp.zeros((16, width), jnp.bfloat16)

    def step(i, total):
        for k in range(8):
            block = magnitude_ref[pl.ds(pl.multiple_of(i * 128 + k * 16, 16), 16), :]
            total = total + jnp.where(block >= bound, one, zero)
        return total

    total = lax.fori_loop(0, rows // 128, step, zero)
    return jnp.sum(total.astype(jnp.float32), axis=0, keepdims=True)


def pick(index, values, other):
    result = jnp.full(index.shape, other, jnp.float32)
    for j, value in enumerate(values):
        result = jnp.where(index == j, value, result)
    return result


def clip_scale(magnitude_ref, edges, limit):
    width = magnitude_ref.shape[1]
    chosen = jnp.zeros((1, width), jnp.int32)
    step = 1
    while step * 2 < len(edges):
        step *= 2
    while step:
        passed = counts(magnitude_ref, pick(chosen + (step - 1), edges, edges[-1])) > limit
        chosen = jnp.where(passed, chosen + step, chosen)
        step //= 2
    upper = pick(chosen, edges, edges[-1])
    lower = pick(chosen - 1, edges, 0.0)
    picked = jnp.zeros((1, width), jnp.int32)

    def level(index):
        part = lower + (upper - lower) * ((index + 1).astype(jnp.float32) / FINE)
        return jnp.where(index >= FINE - 1, upper, part)

    step = FINE // 2
    while step:
        passed = counts(magnitude_ref, level(picked + (step - 1))) > limit
        picked = jnp.where(passed, picked + step, picked)
        step //= 2
    return level(picked)


def local_kernel(bins, edges_ref, x_ref, w_ref, gate_ref, up_ref, out_ref, magnitude, total):
    k = pl.program_id(0)
    named = w_ref[...] > 0.0
    limit = jnp.floor(jnp.sum(named.astype(jnp.float32)) / clip_parts)
    x = x_ref[...]
    magnitude[...] = jnp.where(named, jnp.abs(x.astype(jnp.float32)), 0.0).astype(jnp.bfloat16)
    edges = [edges_ref[j] for j in range(bins)]
    scale = clip_scale(magnitude, edges, limit).astype(jnp.bfloat16)
    x = jnp.minimum(jnp.maximum(x, -scale), scale)
    half = gate_ref.shape[1]

    @pl.when(k == 0)
    def _():
        total[...] = jnp.zeros_like(total)

    total[:, :half] += jnp.dot(x, gate_ref[...], preferred_element_type=jnp.float32)
    total[:, half:] += jnp.dot(x, up_ref[...], preferred_element_type=jnp.float32)

    @pl.when(k == pl.num_programs(0) - 1)
    def _():
        out_ref[...] = total[...].astype(out_ref.dtype)


def local_partial(x, w, gate, up, edges):
    rows, width = x.shape[0], gate.shape[0]
    hidden = gate.shape[1]
    chunk = 512 if width % 512 == 0 else 256
    return pl.pallas_call(
        functools.partial(local_kernel, edges.shape[0]),
        out_shape=jax.ShapeDtypeStruct((rows, 2 * hidden), jnp.bfloat16),
        grid=(width // chunk,),
        in_specs=[
            pl.BlockSpec(memory_space=pltpu.SMEM),
            pl.BlockSpec((rows, chunk), lambda k: (0, k)),
            pl.BlockSpec((rows, 1), lambda k: (0, 0)),
            pl.BlockSpec((chunk, hidden), lambda k: (k, 0)),
            pl.BlockSpec((chunk, hidden), lambda k: (k, 0)),
        ],
        out_specs=pl.BlockSpec((rows, 2 * hidden), lambda k: (0, 0)),
        scratch_shapes=[
            pltpu.VMEM((rows, chunk), jnp.bfloat16),
            pltpu.VMEM((rows, 2 * hidden), jnp.float32),
        ],
        compiler_params=pltpu.CompilerParams(vmem_limit_bytes=60 * 2**20),
    )(edges, x, w, gate, up)


def body(tokens, expert_ids, route_weights, gate_weight, up_weight, down_weight, bin_edges):
    experts = lax.axis_size("expert")
    me = lax.axis_index("expert")
    replicas = lax.axis_size("replica")
    tok_rows, width = tokens.shape
    top = expert_ids.shape[1]
    hidden_units = gate_weight.shape[2]
    share = hidden_units // replicas
    notes = jnp.concatenate([expert_ids.astype(jnp.bfloat16), route_weights], axis=1)
    notes = jnp.pad(notes, ((0, 0), (0, 128 - 2 * top)))
    x = lax.all_gather(jnp.concatenate([tokens, notes], axis=1), "expert", axis=0, tiled=True)
    ids = x[:, width : width + top].astype(jnp.int32)
    w = jnp.sum(
        jnp.where(ids == me, x[:, width + top : width + 2 * top].astype(jnp.float32), 0.0),
        axis=1,
        keepdims=True,
    )
    expert_load = (jnp.sum(w) / (tok_rows * top)).reshape(1)
    partial_value = local_partial(x, w, gate_weight[0], up_weight[0], bin_edges)
    paired = jnp.swapaxes(partial_value.reshape(-1, 2, replicas, share), 1, 2).reshape(
        -1, 2 * hidden_units
    )
    mine = lax.psum_scatter(paired, "replica", scatter_dimension=1, tiled=True).astype(jnp.float32)
    hidden_piece = (jax.nn.silu(mine[:, :share]) * mine[:, share:]).astype(jnp.bfloat16)
    hidden = lax.all_gather(hidden_piece, "replica", axis=1, tiled=True)
    result = jnp.dot(hidden, down_weight[0], preferred_element_type=jnp.float32)
    result = (w * result).astype(jnp.bfloat16)
    mixed = lax.psum_scatter(result, "expert", scatter_dimension=0, tiled=True)
    return (mixed, expert_load)


def solution(mesh):
    return jax.shard_map(
        body,
        mesh=mesh,
        in_specs=(
            P("expert", "replica"),
            P("expert", None),
            P("expert", None),
            P("expert", "replica", None),
            P("expert", "replica", None),
            P("expert", None, "replica"),
            P(),
        ),
        out_specs=(P("expert", "replica"), P("expert")),
        check_vma=False,
    )
```

```python
import functools

import jax
import jax.numpy as jnp
from jax import lax
from jax.experimental import pallas as pl
from jax.experimental.pallas import tpu as pltpu
from jax.sharding import PartitionSpec as P

FINE = 8
clip_parts = 8


def round_up(level):
    near = level.astype(jnp.bfloat16)
    wide = near.astype(jnp.float32)
    above = (wide * (1.0 + 0.75 * 2.0**-7)).astype(jnp.bfloat16)
    return jnp.where(wide < level, above.astype(jnp.float32), wide).astype(jnp.bfloat16)


def counts(magnitude_ref, level):
    rows, width = magnitude_ref.shape
    bound = jnp.broadcast_to(round_up(level), (16, width))
    one, zero = jnp.ones((16, width), jnp.bfloat16), jnp.zeros((16, width), jnp.bfloat16)

    def step(i, total):
        for k in range(8):
            block = magnitude_ref[pl.ds(pl.multiple_of(i * 128 + k * 16, 16), 16), :]
            total = total + jnp.where(block >= bound, one, zero)
        return total

    total = lax.fori_loop(0, rows // 128, step, zero)
    return jnp.sum(total.astype(jnp.float32), axis=0, keepdims=True)


def pick(index, values, other):
    result = jnp.full(index.shape, other, jnp.float32)
    for j, value in enumerate(values):
        result = jnp.where(index == j, value, result)
    return result


def clip_scale(magnitude_ref, edges, limit):
    width = magnitude_ref.shape[1]
    chosen = jnp.zeros((1, width), jnp.int32)
    step = 1
    while step * 2 < len(edges):
        step *= 2
    while step:
        passed = counts(magnitude_ref, pick(chosen + (step - 1), edges, edges[-1])) > limit
        chosen = jnp.where(passed, chosen + step, chosen)
        step //= 2
    upper = pick(chosen, edges, edges[-1])
    lower = pick(chosen - 1, edges, 0.0)
    picked = jnp.zeros((1, width), jnp.int32)

    def level(index):
        part = lower + (upper - lower) * ((index + 1).astype(jnp.float32) / FINE)
        return jnp.where(index >= FINE - 1, upper, part)

    step = FINE // 2
    while step:
        passed = counts(magnitude_ref, level(picked + (step - 1))) > limit
        picked = jnp.where(passed, picked + step, picked)
        step //= 2
    return level(picked)


def local_kernel(bins, edges_ref, x_ref, w_ref, gate_ref, up_ref, out_ref, magnitude, total):
    k = pl.program_id(0)
    named = w_ref[...] > 0.0
    limit = jnp.floor(jnp.sum(named.astype(jnp.float32)) / clip_parts)
    x = x_ref[...]
    magnitude[...] = jnp.where(named, jnp.abs(x.astype(jnp.float32)), 0.0).astype(jnp.bfloat16)
    edges = [edges_ref[j] for j in range(bins)]
    scale = clip_scale(magnitude, edges, limit).astype(jnp.bfloat16)
    x = jnp.minimum(jnp.maximum(x, -scale), scale)
    half = gate_ref.shape[1]

    @pl.when(k == 0)
    def _():
        total[...] = jnp.zeros_like(total)

    total[:, :half] += jnp.dot(x, gate_ref[...], preferred_element_type=jnp.float32)
    total[:, half:] += jnp.dot(x, up_ref[...], preferred_element_type=jnp.float32)

    @pl.when(k == pl.num_programs(0) - 1)
    def _():
        out_ref[...] = total[...].astype(out_ref.dtype)


def local_partial(x, w, gate, up, edges):
    rows, width = x.shape[0], gate.shape[0]
    hidden = gate.shape[1]
    chunk = 512 if width % 512 == 0 else 256
    return pl.pallas_call(
        functools.partial(local_kernel, edges.shape[0]),
        out_shape=jax.ShapeDtypeStruct((rows, 2 * hidden), jnp.bfloat16),
        grid=(width // chunk,),
        in_specs=[
            pl.BlockSpec(memory_space=pltpu.SMEM),
            pl.BlockSpec((rows, chunk), lambda k: (0, k)),
            pl.BlockSpec((rows, 1), lambda k: (0, 0)),
            pl.BlockSpec((chunk, hidden), lambda k: (k, 0)),
            pl.BlockSpec((chunk, hidden), lambda k: (k, 0)),
        ],
        out_specs=pl.BlockSpec((rows, 2 * hidden), lambda k: (0, 0)),
        scratch_shapes=[
            pltpu.VMEM((rows, chunk), jnp.bfloat16),
            pltpu.VMEM((rows, 2 * hidden), jnp.float32),
        ],
        compiler_params=pltpu.CompilerParams(vmem_limit_bytes=60 * 2**20),
    )(edges, x, w, gate, up)


MESH = pl.DeviceIdType.MESH
NOTE = 128
KC = 4
VMEM_MOST = 67043328


def fused_kernel(
    bins, top, x_hbm, gate_hbm, up_hbm, down_hbm, edges_ref, out_ref, load_ref,
    xg, mag, wv, gu, down, sbuf, rbuf, own, hid, outb, sibr, scw, rcw, sccw, rccw,
    load_sems, ring_send, ring_recv, sib_send, sib_recv, part_send, part_recv,
    hid_send, hid_recv, pair_send, pair_recv, cw_send, cw_recv, ccw_send, ccw_recv,
):
    experts = lax.axis_size("expert")
    me, r = lax.axis_index("expert"), lax.axis_index("replica")
    chips = experts // 2
    half_ring = chips // 2
    c = lax.rem(me, 2)
    chip = lax.div(me, 2)
    odd, low = lax.rem(chip, 2), lax.div(chip, 2)
    pos = (1 - odd) * low + odd * (chips - 1 - low)

    def at(place):
        place = lax.rem(place + chips, chips)
        back = lax.div(place, half_ring)
        number = (1 - back) * (2 * place) + back * (2 * (chips - 1 - place) + 1)
        return (number * 2 + c, r)

    right, left = at(pos + 1), at(pos - 1)
    sibling = (chip * 2 + (1 - c), r)
    partner = (me, 1 - r)

    rows, wide = xg.shape
    tok = rows // experts
    width = wide - NOTE
    share = hid.shape[1] // 2
    tile = own.shape[2]
    tiles = own.shape[0]
    blocks = half_ring
    brows = rows // blocks

    own_load = pltpu.make_async_copy(
        x_hbm, xg.at[pl.ds(pl.multiple_of(((chips - 1) * 2 + c) * tok, tok), tok), :], load_sems.at[0]
    )
    own_load.start()
    weight_loads = [
        pltpu.make_async_copy(gate_hbm, gu.at[0], load_sems.at[1]),
        pltpu.make_async_copy(up_hbm, gu.at[1], load_sems.at[2]),
        pltpu.make_async_copy(down_hbm, down, load_sems.at[3]),
    ]
    for copy in weight_loads:
        copy.start()

    barrier = pltpu.get_barrier_semaphore()
    for other in (right, left, sibling, partner):
        pl.semaphore_signal(barrier, inc=1, device_id=other, device_id_type=MESH)
    pl.semaphore_wait(barrier, 4)
    own_load.wait()

    def slot(distance):
        if distance == 0:
            return chips - 1
        if distance == half_ring or distance == -half_ring:
            return chips - 2
        return 2 * (distance - 1) if distance > 0 else 2 * (-distance - 1) + 1

    def block(s, core, k):
        step = width // KC
        begin, size = (0, NOTE + step) if k == 0 else (NOTE + k * step, step)
        start = pl.multiple_of((s * 2 + core) * tok, tok)
        return xg.at[pl.ds(start, tok), pl.ds(begin, size)]

    def ring_copy(distance, k, way):
        nearer = slot(distance)
        further = slot(distance + way)
        return pltpu.make_async_remote_copy(
            src_ref=block(nearer, c, k), dst_ref=block(further, c, k),
            send_sem=ring_send.at[k, 0 if way > 0 else 1, abs(distance)],
            recv_sem=ring_recv.at[k, further],
            device_id=right if way > 0 else left, device_id_type=MESH,
        )

    def sib_copy(s, k):
        return pltpu.make_async_remote_copy(
            src_ref=block(s, c, k), dst_ref=block(s, c, k),
            send_sem=sib_send.at[k, s], recv_sem=sib_recv.at[k, s],
            device_id=sibling, device_id_type=MESH,
        )

    def sib_arrival(s, k):
        return pltpu.make_async_remote_copy(
            src_ref=block(s, 1 - c, k), dst_ref=block(s, 1 - c, k),
            send_sem=sib_send.at[k, s], recv_sem=sib_recv.at[k, s],
            device_id=sibling, device_id_type=MESH,
        )

    started = []
    events = sorted((h + 2 * k, k, h) for k in range(KC) for h in range(half_ring + 1))
    for _, k, h in events:
        for way in (1, -1):
            hops = half_ring if (way > 0) == (k % 2 == 0) else half_ring - 1
            if h > hops:
                continue
            if h > 0:
                ring_copy(way * (h - 1), k, way).wait_recv()
            if h < hops:
                copy = ring_copy(way * h, k, way)
                copy.start()
                started.append(copy)
            if h > 0 or way > 0:
                copy = sib_copy(slot(way * h), k)
                copy.start()
                started.append(copy)
    for k in range(KC):
        for s in range(chips):
            sib_arrival(s, k).wait_recv()
    for copy in started:
        copy.wait_send()

    lane = lax.broadcasted_iota(jnp.int32, (rows, NOTE), 1)
    wv[...] = jnp.sum(
        jnp.where(lane == me, xg[:, 0:NOTE].astype(jnp.float32), 0.0), axis=1, keepdims=True
    )
    load_ref[...] = jnp.full(load_ref.shape, jnp.sum(wv[...]) / (tok * top), jnp.float32)
    limit = jnp.floor(jnp.sum((wv[...] > 0.0).astype(jnp.float32)) / clip_parts)
    edges = [edges_ref[j] for j in range(bins)]
    chunk = mag.shape[1]

    def clip_step(k, carry):
        columns = pl.ds(pl.multiple_of(NOTE + k * chunk, 128), chunk)
        x = xg[:, columns]
        mag[...] = jnp.where(wv[...] > 0.0, jnp.abs(x.astype(jnp.float32)), 0.0).astype(jnp.bfloat16)
        scale = clip_scale(mag, edges, limit).astype(jnp.bfloat16)
        xg[:, columns] = jnp.minimum(jnp.maximum(xg[:, columns], -scale), scale)
        return carry

    lax.fori_loop(0, width // chunk, clip_step, 0)

    weight_loads[0].wait()
    weight_loads[1].wait()
    per = tiles // 2

    def product(j, side):
        begin = pl.multiple_of(side * share + lax.rem(j, per) * tile, 128)
        return jnp.dot(
            xg[:, NOTE:], gu[lax.div(j, per), :, pl.ds(begin, tile)],
            preferred_element_type=jnp.float32,
        )

    def part_copy(j, i):
        span = pl.ds(pl.multiple_of(i * brows, brows), brows)
        return pltpu.make_async_remote_copy(
            src_ref=sbuf.at[j, span, :], dst_ref=rbuf.at[j, span, :],
            send_sem=part_send.at[j, i], recv_sem=part_recv.at[j, i],
            device_id=partner, device_id_type=MESH,
        )

    def send_step(j, carry):
        sbuf[j] = product(j, 1 - r).astype(jnp.bfloat16)
        for i in range(blocks):
            part_copy(j, i).start()
        return carry

    def keep_step(j, carry):
        own[j] = product(j, r)
        return carry

    lax.fori_loop(0, tiles, send_step, 0)
    lax.fori_loop(0, tiles, keep_step, 0)

    def hid_copy(i, side):
        place = hid.at[
            pl.ds(pl.multiple_of(i * brows, brows), brows),
            pl.ds(pl.multiple_of(side * share, 128), share),
        ]
        return pltpu.make_async_remote_copy(
            src_ref=place, dst_ref=place, send_sem=hid_send.at[i], recv_sem=hid_recv.at[i],
            device_id=partner, device_id_type=MESH,
        )

    def hidden_step(i, carry):
        span = pl.ds(pl.multiple_of(i * brows, brows), brows)
        for j in range(tiles):
            part_copy(j, i).wait_recv()
        for j in range(per):
            gate = own[j, span, :] + rbuf[j, span, :].astype(jnp.float32)
            up = own[j + per, span, :] + rbuf[j + per, span, :].astype(jnp.float32)
            place = pl.ds(pl.multiple_of(r * share + j * tile, 128), tile)
            hid[span, place] = (gate / (1.0 + jnp.exp(-gate)) * up).astype(jnp.bfloat16)
        hid_copy(i, r).start()
        return carry

    lax.fori_loop(0, blocks, hidden_step, 0)

    weight_loads[2].wait()
    middle = width // 2

    def pair_copy(s):
        span = pl.ds(pl.multiple_of((s * 2 + (1 - c)) * tok, tok), tok)
        return pltpu.make_async_remote_copy(
            src_ref=outb.at[span, :], dst_ref=sibr.at[s],
            send_sem=pair_send.at[s], recv_sem=pair_recv.at[s],
            device_id=sibling, device_id_type=MESH,
        )

    def cw_copy(s):
        return pltpu.make_async_remote_copy(
            src_ref=scw.at[s], dst_ref=rcw.at[s], send_sem=cw_send.at[s], recv_sem=cw_recv.at[s],
            device_id=right, device_id_type=MESH,
        )

    def ccw_copy(s):
        return pltpu.make_async_remote_copy(
            src_ref=sccw.at[s], dst_ref=rccw.at[s], send_sem=ccw_send.at[s], recv_sem=ccw_recv.at[s],
            device_id=left, device_id_type=MESH,
        )

    def share_of(s, begin):
        span = pl.ds(pl.multiple_of((s * 2 + c) * tok, tok), tok)
        mine = outb[span, begin : begin + middle].astype(jnp.float32)
        return mine + sibr[s, :, begin : begin + middle].astype(jnp.float32)

    def ring_step(s, cw_slot, ccw_slot):
        cw_copy(s - 1).wait_recv()
        scw[s] = (share_of(cw_slot, 0) + rcw[s - 1].astype(jnp.float32)).astype(jnp.bfloat16)
        cw_copy(s).start()
        ccw_copy(s - 1).wait_recv()
        sccw[s] = (share_of(ccw_slot, middle) + rccw[s - 1].astype(jnp.float32)).astype(jnp.bfloat16)
        ccw_copy(s).start()

    piece = 512 if width % 512 == 0 else 128

    def down_step(i, carry):
        span = pl.ds(pl.multiple_of(i * brows, brows), brows)
        hid_copy(i, 1 - r).wait_recv()

        def columns_step(n, carry):
            columns = pl.ds(pl.multiple_of(n * piece, 128), piece)
            result = jnp.dot(hid[span, :], down[:, columns], preferred_element_type=jnp.float32)
            outb[span, columns] = (wv[span, :] * result).astype(jnp.bfloat16)
            return carry

        lax.fori_loop(0, width // piece, columns_step, 0)
        pair_copy(2 * i).start()
        pair_copy(2 * i + 1).start()
        pair_copy(2 * i).wait_recv()
        pair_copy(2 * i + 1).wait_recv()

        @pl.when(i == 0)
        def _():
            scw[0] = share_of(0, 0).astype(jnp.bfloat16)
            cw_copy(0).start()
            sccw[0] = share_of(1, middle).astype(jnp.bfloat16)
            ccw_copy(0).start()

        @pl.when(i > 0)
        def _():
            ring_step(i, 2 * i, jnp.minimum(2 * i + 1, chips - 2))

        return carry

    lax.fori_loop(0, blocks, down_step, 0)
    for s in range(half_ring, chips - 1):
        back = 2 * (s - half_ring)
        ring_step(s, chips - 3 - back, chips - 4 - back)
    cw_copy(chips - 2).wait_recv()
    out_ref[:, :middle] = (
        share_of(chips - 1, 0) + rcw[chips - 2].astype(jnp.float32)
    ).astype(out_ref.dtype)
    ccw_copy(chips - 2).wait_recv()
    out_ref[:, middle:] = (
        share_of(chips - 1, middle) + rccw[chips - 2].astype(jnp.float32)
    ).astype(out_ref.dtype)
    for i in range(blocks):
        for j in range(tiles):
            part_copy(j, i).wait_send()
        hid_copy(i, r).wait_send()
    for s in range(chips):
        pair_copy(s).wait_send()
    for s in range(chips - 1):
        cw_copy(s).wait_send()
        ccw_copy(s).wait_send()


def fused_scratch(experts, tok, width, hidden):
    rows, chips = experts * tok, experts // 2
    share = hidden // 2
    tile = 256 if share % 256 == 0 else 128
    tiles = 2 * share // tile
    chunk = 512 if width % 512 == 0 else 128
    bf, f32 = jnp.bfloat16, jnp.float32
    ring = (chips - 1, tok, width // 2)
    return [
        ((rows, NOTE + width), bf), ((rows, chunk), bf), ((rows, 1), f32),
        ((2, width, hidden), bf), ((hidden, width), bf),
        ((tiles, rows, tile), bf), ((tiles, rows, tile), bf), ((tiles, rows, tile), f32),
        ((rows, hidden), bf), ((rows, width), bf), ((chips, tok, width), bf),
        (ring, bf), (ring, bf), (ring, bf), (ring, bf),
    ]


def fused_fits(experts, replicas, tok, width, hidden):
    held = 0
    for shape, dtype in fused_scratch(experts, tok, width, hidden):
        size = jnp.dtype(dtype).itemsize
        for n in shape[:-1] + (max(shape[-1], 128),):
            size *= n
        held += size
    even = experts % 4 == 0 and replicas == 2 and tok % 16 == 0 and experts <= NOTE
    return even and width % (KC * 128) == 0 and held < 0.9 * VMEM_MOST


def fused(x, gate, up, down, edges, experts, top):
    tok, wide = x.shape
    width, hidden = gate.shape
    chips = experts // 2
    shapes = fused_scratch(experts, tok, width, hidden)
    tiles, blocks = shapes[5][0][0], chips // 2
    dma = pltpu.SemaphoreType.DMA
    any_spec = pl.BlockSpec(memory_space=pl.ANY)
    vmem = pl.BlockSpec(memory_space=pltpu.VMEM)
    return pl.pallas_call(
        functools.partial(fused_kernel, edges.shape[0], top),
        out_shape=(
            jax.ShapeDtypeStruct((tok, width), jnp.bfloat16),
            jax.ShapeDtypeStruct((1, 128), jnp.float32),
        ),
        in_specs=[any_spec] * 4 + [pl.BlockSpec(memory_space=pltpu.SMEM)],
        out_specs=(vmem, vmem),
        scratch_shapes=[pltpu.VMEM(shape, dtype) for shape, dtype in shapes]
        + [
            dma((4,)), dma((KC, 2, blocks)), dma((KC, chips)), dma((KC, chips)), dma((KC, chips)),
            dma((tiles, blocks)), dma((tiles, blocks)), dma((blocks,)), dma((blocks,)),
            dma((chips,)), dma((chips,)), dma((chips - 1,)), dma((chips - 1,)),
            dma((chips - 1,)), dma((chips - 1,)),
        ],
        compiler_params=pltpu.CompilerParams(
            collective_id=0, has_side_effects=True, vmem_limit_bytes=VMEM_MOST
        ),
    )(x, gate, up, down, edges)


def body(tokens, expert_ids, route_weights, gate_weight, up_weight, down_weight, bin_edges):
    experts = lax.axis_size("expert")
    me = lax.axis_index("expert")
    replicas = lax.axis_size("replica")
    tok_rows, width = tokens.shape
    top = expert_ids.shape[1]
    hidden_units = gate_weight.shape[2]
    share = hidden_units // replicas
    if fused_fits(experts, replicas, tok_rows, width, hidden_units):
        numbers = jnp.arange(NOTE, dtype=jnp.int32)
        notes = sum(
            jnp.where(expert_ids[:, k : k + 1] == numbers, route_weights[:, k : k + 1], 0)
            for k in range(top)
        )
        mixed, load = fused(
            jnp.concatenate([notes.astype(jnp.bfloat16), tokens], axis=1),
            gate_weight[0], up_weight[0], down_weight[0], bin_edges, experts, top,
        )
        return mixed, load[0, :1]
    notes = jnp.concatenate([expert_ids.astype(jnp.bfloat16), route_weights], axis=1)
    notes = jnp.pad(notes, ((0, 0), (0, 128 - 2 * top)))
    x = lax.all_gather(jnp.concatenate([tokens, notes], axis=1), "expert", axis=0, tiled=True)
    ids = x[:, width : width + top].astype(jnp.int32)
    w = jnp.sum(
        jnp.where(ids == me, x[:, width + top : width + 2 * top].astype(jnp.float32), 0.0),
        axis=1,
        keepdims=True,
    )
    expert_load = (jnp.sum(w) / (tok_rows * top)).reshape(1)
    partial_value = local_partial(x, w, gate_weight[0], up_weight[0], bin_edges)
    paired = jnp.swapaxes(partial_value.reshape(-1, 2, replicas, share), 1, 2).reshape(
        -1, 2 * hidden_units
    )
    mine = lax.psum_scatter(paired, "replica", scatter_dimension=1, tiled=True).astype(jnp.float32)
    hidden_piece = (jax.nn.silu(mine[:, :share]) * mine[:, share:]).astype(jnp.bfloat16)
    hidden = lax.all_gather(hidden_piece, "replica", axis=1, tiled=True)
    result = jnp.dot(hidden, down_weight[0], preferred_element_type=jnp.float32)
    result = (w * result).astype(jnp.bfloat16)
    mixed = lax.psum_scatter(result, "expert", scatter_dimension=0, tiled=True)
    return (mixed, expert_load)


def solution(mesh):
    return jax.shard_map(
        body,
        mesh=mesh,
        in_specs=(
            P("expert", "replica"),
            P("expert", None),
            P("expert", None),
            P("expert", "replica", None),
            P("expert", "replica", None),
            P("expert", None, "replica"),
            P(),
        ),
        out_specs=(P("expert", "replica"), P("expert")),
        check_vma=False,
    )
```

```python
import functools

import jax
import jax.numpy as jnp
from jax import lax
from jax.experimental import pallas as pl
from jax.experimental.pallas import tpu as pltpu
from jax.sharding import PartitionSpec as P

FINE = 8
clip_parts = 8


def round_up(level):
    near = level.astype(jnp.bfloat16)
    wide = near.astype(jnp.float32)
    above = (wide * (1.0 + 0.75 * 2.0**-7)).astype(jnp.bfloat16)
    return jnp.where(wide < level, above.astype(jnp.float32), wide).astype(jnp.bfloat16)


def counts(magnitude_ref, level):
    rows, width = magnitude_ref.shape
    bound = jnp.broadcast_to(round_up(level), (16, width))
    one, zero = jnp.ones((16, width), jnp.bfloat16), jnp.zeros((16, width), jnp.bfloat16)

    def step(i, total):
        for k in range(8):
            block = magnitude_ref[pl.ds(pl.multiple_of(i * 128 + k * 16, 16), 16), :]
            total = total + jnp.where(block >= bound, one, zero)
        return total

    total = lax.fori_loop(0, rows // 128, step, zero)
    return jnp.sum(total.astype(jnp.float32), axis=0, keepdims=True)


def pick(index, values, other):
    result = jnp.full(index.shape, other, jnp.float32)
    for j, value in enumerate(values):
        result = jnp.where(index == j, value, result)
    return result


def clip_scale(magnitude_ref, edges, limit):
    width = magnitude_ref.shape[1]
    chosen = jnp.zeros((1, width), jnp.int32)
    step = 1
    while step * 2 < len(edges):
        step *= 2
    while step:
        passed = counts(magnitude_ref, pick(chosen + (step - 1), edges, edges[-1])) > limit
        chosen = jnp.where(passed, chosen + step, chosen)
        step //= 2
    upper = pick(chosen, edges, edges[-1])
    lower = pick(chosen - 1, edges, 0.0)
    picked = jnp.zeros((1, width), jnp.int32)

    def level(index):
        part = lower + (upper - lower) * ((index + 1).astype(jnp.float32) / FINE)
        return jnp.where(index >= FINE - 1, upper, part)

    step = FINE // 2
    while step:
        passed = counts(magnitude_ref, level(picked + (step - 1))) > limit
        picked = jnp.where(passed, picked + step, picked)
        step //= 2
    return level(picked)


def local_kernel(bins, edges_ref, x_ref, w_ref, gate_ref, up_ref, out_ref, magnitude, total):
    k = pl.program_id(0)
    named = w_ref[...] > 0.0
    limit = jnp.floor(jnp.sum(named.astype(jnp.float32)) / clip_parts)
    x = x_ref[...]
    magnitude[...] = jnp.where(named, jnp.abs(x.astype(jnp.float32)), 0.0).astype(jnp.bfloat16)
    edges = [edges_ref[j] for j in range(bins)]
    scale = clip_scale(magnitude, edges, limit).astype(jnp.bfloat16)
    x = jnp.minimum(jnp.maximum(x, -scale), scale)
    half = gate_ref.shape[1]

    @pl.when(k == 0)
    def _():
        total[...] = jnp.zeros_like(total)

    total[:, :half] += jnp.dot(x, gate_ref[...], preferred_element_type=jnp.float32)
    total[:, half:] += jnp.dot(x, up_ref[...], preferred_element_type=jnp.float32)

    @pl.when(k == pl.num_programs(0) - 1)
    def _():
        out_ref[...] = total[...].astype(out_ref.dtype)


def local_partial(x, w, gate, up, edges):
    rows, width = x.shape[0], gate.shape[0]
    hidden = gate.shape[1]
    chunk = 512 if width % 512 == 0 else 256
    return pl.pallas_call(
        functools.partial(local_kernel, edges.shape[0]),
        out_shape=jax.ShapeDtypeStruct((rows, 2 * hidden), jnp.bfloat16),
        grid=(width // chunk,),
        in_specs=[
            pl.BlockSpec(memory_space=pltpu.SMEM),
            pl.BlockSpec((rows, chunk), lambda k: (0, k)),
            pl.BlockSpec((rows, 1), lambda k: (0, 0)),
            pl.BlockSpec((chunk, hidden), lambda k: (k, 0)),
            pl.BlockSpec((chunk, hidden), lambda k: (k, 0)),
        ],
        out_specs=pl.BlockSpec((rows, 2 * hidden), lambda k: (0, 0)),
        scratch_shapes=[
            pltpu.VMEM((rows, chunk), jnp.bfloat16),
            pltpu.VMEM((rows, 2 * hidden), jnp.float32),
        ],
        compiler_params=pltpu.CompilerParams(vmem_limit_bytes=60 * 2**20),
    )(edges, x, w, gate, up)


MESH = pl.DeviceIdType.MESH
NOTE = 128
KC = 4
VMEM_MOST = 67043328


def fused_kernel(
    bins, top, x_hbm, gate_hbm, up_hbm, down_hbm, edges_ref, out_ref, load_ref,
    xg, mag, wv, gu, down, sbuf, rbuf, own, hid, outb, sibr, scw, rcw, sccw, rccw,
    load_sems, ring_send, ring_recv, sib_send, sib_recv, part_send, part_recv,
    hid_send, hid_recv, pair_send, pair_recv, cw_send, cw_recv, ccw_send, ccw_recv,
):
    experts = lax.axis_size("expert")
    me, r = lax.axis_index("expert"), lax.axis_index("replica")
    chips = experts // 2
    half_ring = chips // 2
    c = lax.rem(me, 2)
    chip = lax.div(me, 2)
    odd, low = lax.rem(chip, 2), lax.div(chip, 2)
    pos = (1 - odd) * low + odd * (chips - 1 - low)

    def at(place):
        place = lax.rem(place + chips, chips)
        back = lax.div(place, half_ring)
        number = (1 - back) * (2 * place) + back * (2 * (chips - 1 - place) + 1)
        return (number * 2 + c, r)

    right, left = at(pos + 1), at(pos - 1)
    sibling = (chip * 2 + (1 - c), r)
    partner = (me, 1 - r)

    rows, wide = xg.shape
    tok = rows // experts
    width = wide - NOTE
    share = hid.shape[1] // 2
    tile = own.shape[2]
    tiles = own.shape[0]
    blocks = half_ring
    brows = rows // blocks

    own_load = pltpu.make_async_copy(
        x_hbm, xg.at[pl.ds(pl.multiple_of((2 + c) * tok, tok), tok), :], load_sems.at[0]
    )
    own_load.start()
    weight_loads = [
        pltpu.make_async_copy(gate_hbm, gu.at[0], load_sems.at[1]),
        pltpu.make_async_copy(up_hbm, gu.at[1], load_sems.at[2]),
        pltpu.make_async_copy(down_hbm, down, load_sems.at[3]),
    ]
    for copy in weight_loads:
        copy.start()

    barrier = pltpu.get_barrier_semaphore()
    for other in (right, left, sibling, partner):
        pl.semaphore_signal(barrier, inc=1, device_id=other, device_id_type=MESH)
    pl.semaphore_wait(barrier, 4)
    own_load.wait()

    def slot(distance):
        if distance == 0:
            return 1
        if abs(distance) == half_ring:
            return 0
        return 2 * (half_ring - abs(distance)) + (0 if distance > 0 else 1)

    def block(s, core, k):
        step = width // KC
        begin, size = (0, NOTE + step) if k == 0 else (NOTE + k * step, step)
        start = pl.multiple_of((s * 2 + core) * tok, tok)
        return xg.at[pl.ds(start, tok), pl.ds(begin, size)]

    def ring_copy(distance, k, way):
        nearer = slot(distance)
        further = slot(distance + way)
        return pltpu.make_async_remote_copy(
            src_ref=block(nearer, c, k), dst_ref=block(further, c, k),
            send_sem=ring_send.at[k, 0 if way > 0 else 1, abs(distance)],
            recv_sem=ring_recv.at[k, further],
            device_id=right if way > 0 else left, device_id_type=MESH,
        )

    def sib_copy(s, k):
        return pltpu.make_async_remote_copy(
            src_ref=block(s, c, k), dst_ref=block(s, c, k),
            send_sem=sib_send.at[k, s], recv_sem=sib_recv.at[k, s],
            device_id=sibling, device_id_type=MESH,
        )

    def sib_arrival(s, k):
        return pltpu.make_async_remote_copy(
            src_ref=block(s, 1 - c, k), dst_ref=block(s, 1 - c, k),
            send_sem=sib_send.at[k, s], recv_sem=sib_recv.at[k, s],
            device_id=sibling, device_id_type=MESH,
        )

    started = []
    events = sorted((h + k, k, h) for k in range(KC) for h in range(half_ring + 1))
    for _, k, h in events:
        for way in (1, -1):
            hops = half_ring if (way > 0) == (k % 2 == 0) else half_ring - 1
            if h > hops:
                continue
            if h > 0:
                ring_copy(way * (h - 1), k, way).wait_recv()
            if h < hops:
                copy = ring_copy(way * h, k, way)
                copy.start()
                started.append(copy)
            if h > 0 or way > 0:
                copy = sib_copy(slot(way * h), k)
                copy.start()
                started.append(copy)
    for k in range(KC):
        for s in range(chips):
            sib_arrival(s, k).wait_recv()
    for copy in started:
        copy.wait_send()

    lane = lax.broadcasted_iota(jnp.int32, (rows, NOTE), 1)
    wv[...] = jnp.sum(
        jnp.where(lane == me, xg[:, 0:NOTE].astype(jnp.float32), 0.0), axis=1, keepdims=True
    )
    load_ref[...] = jnp.full(load_ref.shape, jnp.sum(wv[...]) / (tok * top), jnp.float32)
    limit = jnp.floor(jnp.sum((wv[...] > 0.0).astype(jnp.float32)) / clip_parts)
    edges = [edges_ref[j] for j in range(bins)]
    chunk = mag.shape[1]

    def clip_step(k, carry):
        columns = pl.ds(pl.multiple_of(NOTE + k * chunk, 128), chunk)
        x = xg[:, columns]
        mag[...] = jnp.where(wv[...] > 0.0, jnp.abs(x.astype(jnp.float32)), 0.0).astype(jnp.bfloat16)
        scale = clip_scale(mag, edges, limit).astype(jnp.bfloat16)
        xg[:, columns] = jnp.minimum(jnp.maximum(xg[:, columns], -scale), scale)
        return carry

    lax.fori_loop(0, width // chunk, clip_step, 0)

    weight_loads[0].wait()
    weight_loads[1].wait()
    per = tiles // 2

    def product(j, side, span):
        begin = pl.multiple_of(side * share + lax.rem(j, per) * tile, 128)
        return jnp.dot(
            xg[span, NOTE:], gu[lax.div(j, per), :, pl.ds(begin, tile)],
            preferred_element_type=jnp.float32,
        )

    def part_copy(j, i):
        span = pl.ds(pl.multiple_of(i * brows, brows), brows)
        return pltpu.make_async_remote_copy(
            src_ref=sbuf.at[j, span, :], dst_ref=rbuf.at[j, span, :],
            send_sem=part_send.at[j, i], recv_sem=part_recv.at[j, i],
            device_id=partner, device_id_type=MESH,
        )

    def hid_copy(i, side):
        place = hid.at[
            pl.ds(pl.multiple_of(i * brows, brows), brows),
            pl.ds(pl.multiple_of(side * share, 128), share),
        ]
        return pltpu.make_async_remote_copy(
            src_ref=place, dst_ref=place, send_sem=hid_send.at[i], recv_sem=hid_recv.at[i],
            device_id=partner, device_id_type=MESH,
        )

    middle = width // 2

    def pair_copy(s):
        span = pl.ds(pl.multiple_of((s * 2 + (1 - c)) * tok, tok), tok)
        return pltpu.make_async_remote_copy(
            src_ref=outb.at[span, :], dst_ref=sibr.at[s],
            send_sem=pair_send.at[s], recv_sem=pair_recv.at[s],
            device_id=sibling, device_id_type=MESH,
        )

    def sum_copy(sent, came, send_sem, recv_sem, s, first, target):
        cols = pl.ds(first, middle) if s == 0 else pl.ds(0, width)
        return pltpu.make_async_remote_copy(
            src_ref=sent.at[s, :, cols], dst_ref=came.at[s, :, cols],
            send_sem=send_sem.at[s], recv_sem=recv_sem.at[s],
            device_id=target, device_id_type=MESH,
        )

    def cw_copy(s):
        return sum_copy(scw, rcw, cw_send, cw_recv, s, 0, right)

    def ccw_copy(s):
        return sum_copy(sccw, rccw, ccw_send, ccw_recv, s, middle, left)

    def share_of(s, begin, size):
        span = pl.ds(pl.multiple_of((s * 2 + c) * tok, tok), tok)
        mine = outb[span, begin : begin + size].astype(jnp.float32)
        return mine + sibr[s, :, begin : begin + size].astype(jnp.float32)

    def stage_send(i):
        span = pl.ds(i * brows, brows)

        def step(j, carry):
            sbuf[j, span, :] = product(j, 1 - r, span).astype(jnp.bfloat16)
            part_copy(j, i).start()
            return carry

        lax.fori_loop(0, tiles, step, 0)

    def stage_hidden(i):
        span = pl.ds(i * brows, brows)

        def step(j, carry):
            own[j, span, :] = product(j, r, span)
            return carry

        lax.fori_loop(0, tiles, step, 0)
        for j in range(tiles):
            part_copy(j, i).wait_recv()
        for j in range(per):
            gate = own[j, span, :] + rbuf[j, span, :].astype(jnp.float32)
            up = own[j + per, span, :] + rbuf[j + per, span, :].astype(jnp.float32)
            place = pl.ds(pl.multiple_of(r * share + j * tile, 128), tile)
            hid[span, place] = (gate / (1.0 + jnp.exp(-gate)) * up).astype(jnp.bfloat16)
        hid_copy(i, r).start()

    piece = 512 if width % 512 == 0 else 128

    def stage_down(i):
        span = pl.ds(i * brows, brows)
        hid_copy(i, 1 - r).wait_recv()
        if i == 0:
            weight_loads[2].wait()

        def step(n, carry):
            columns = pl.ds(pl.multiple_of(n * piece, 128), piece)
            result = jnp.dot(hid[span, :], down[:, columns], preferred_element_type=jnp.float32)
            outb[span, columns] = (wv[span, :] * result).astype(jnp.bfloat16)
            return carry

        lax.fori_loop(0, width // piece, step, 0)
        pair_copy(2 * i).start()
        pair_copy(2 * i + 1).start()
        pair_copy(2 * i).wait_recv()
        pair_copy(2 * i + 1).wait_recv()
        for sums, came, copy, s, first in (
            (scw, rcw, cw_copy, 2 * i + 1 if i else 0, 0),
            (sccw, rccw, ccw_copy, 2 * i, middle),
        ):
            if i:
                copy(i - 1).wait_recv()
            for begin in (0, middle):
                cols = slice(begin, begin + middle)
                if i == 0 and begin != first:
                    continue
                value = share_of(s, begin, middle)
                if i > 1 or (i == 1 and begin == first):
                    value = value + came[i - 1, :, cols].astype(jnp.float32)
                sums[i, :, cols] = value.astype(jnp.bfloat16)
            copy(i).start()

    for t in range(blocks + 2):
        if t < blocks:
            stage_send(t)
        if 1 <= t <= blocks:
            stage_hidden(t - 1)
        if t >= 2:
            stage_down(t - 2)
    last = blocks - 1
    cw_copy(last).wait_recv()
    ccw_copy(last).wait_recv()
    for begin in (0, middle):
        cols = slice(begin, begin + middle)
        value = share_of(1, begin, middle) + rcw[last, :, cols].astype(jnp.float32)
        out_ref[:, cols] = (value + rccw[last, :, cols].astype(jnp.float32)).astype(out_ref.dtype)
    for i in range(blocks):
        for j in range(tiles):
            part_copy(j, i).wait_send()
        hid_copy(i, r).wait_send()
        cw_copy(i).wait_send()
        ccw_copy(i).wait_send()
    for s in range(chips):
        pair_copy(s).wait_send()


def fused_scratch(experts, tok, width, hidden):
    rows, chips = experts * tok, experts // 2
    share = hidden // 2
    tile = 256 if share % 256 == 0 else 128
    tiles = 2 * share // tile
    chunk = 512 if width % 512 == 0 else 128
    bf, f32 = jnp.bfloat16, jnp.float32
    ring = (chips // 2, tok, width)
    return [
        ((rows, NOTE + width), bf), ((rows, chunk), bf), ((rows, 1), f32),
        ((2, width, hidden), bf), ((hidden, width), bf),
        ((tiles, rows, tile), bf), ((tiles, rows, tile), bf), ((tiles, rows, tile), f32),
        ((rows, hidden), bf), ((rows, width), bf), ((chips, tok, width), bf),
        (ring, bf), (ring, bf), (ring, bf), (ring, bf),
    ]


def fused_fits(experts, replicas, tok, width, hidden):
    held = 0
    for shape, dtype in fused_scratch(experts, tok, width, hidden):
        size = jnp.dtype(dtype).itemsize
        for n in shape[:-1] + (max(shape[-1], 128),):
            size *= n
        held += size
    even = experts % 4 == 0 and replicas == 2 and tok % 16 == 0 and experts <= NOTE
    return even and width % (KC * 128) == 0 and held < 0.9 * VMEM_MOST


def fused(x, gate, up, down, edges, experts, top):
    tok, wide = x.shape
    width, hidden = gate.shape
    chips = experts // 2
    shapes = fused_scratch(experts, tok, width, hidden)
    tiles, blocks = shapes[5][0][0], chips // 2
    dma = pltpu.SemaphoreType.DMA
    any_spec = pl.BlockSpec(memory_space=pl.ANY)
    vmem = pl.BlockSpec(memory_space=pltpu.VMEM)
    return pl.pallas_call(
        functools.partial(fused_kernel, edges.shape[0], top),
        out_shape=(
            jax.ShapeDtypeStruct((tok, width), jnp.bfloat16),
            jax.ShapeDtypeStruct((1, 128), jnp.float32),
        ),
        in_specs=[any_spec] * 4 + [pl.BlockSpec(memory_space=pltpu.SMEM)],
        out_specs=(vmem, vmem),
        scratch_shapes=[pltpu.VMEM(shape, dtype) for shape, dtype in shapes]
        + [
            dma((4,)), dma((KC, 2, blocks)), dma((KC, chips)), dma((KC, chips)), dma((KC, chips)),
            dma((tiles, blocks)), dma((tiles, blocks)), dma((blocks,)), dma((blocks,)),
            dma((chips,)), dma((chips,)), dma((blocks,)), dma((blocks,)),
            dma((blocks,)), dma((blocks,)),
        ],
        compiler_params=pltpu.CompilerParams(
            collective_id=0, has_side_effects=True, vmem_limit_bytes=VMEM_MOST
        ),
    )(x, gate, up, down, edges)


def body(tokens, expert_ids, route_weights, gate_weight, up_weight, down_weight, bin_edges):
    experts = lax.axis_size("expert")
    me = lax.axis_index("expert")
    replicas = lax.axis_size("replica")
    tok_rows, width = tokens.shape
    top = expert_ids.shape[1]
    hidden_units = gate_weight.shape[2]
    share = hidden_units // replicas
    if fused_fits(experts, replicas, tok_rows, width, hidden_units):
        numbers = jnp.arange(NOTE, dtype=jnp.int32)
        notes = sum(
            jnp.where(expert_ids[:, k : k + 1] == numbers, route_weights[:, k : k + 1], 0)
            for k in range(top)
        )
        mixed, load = fused(
            jnp.concatenate([notes.astype(jnp.bfloat16), tokens], axis=1),
            gate_weight[0], up_weight[0], down_weight[0], bin_edges, experts, top,
        )
        return mixed, load[0, :1]
    notes = jnp.concatenate([expert_ids.astype(jnp.bfloat16), route_weights], axis=1)
    notes = jnp.pad(notes, ((0, 0), (0, 128 - 2 * top)))
    x = lax.all_gather(jnp.concatenate([tokens, notes], axis=1), "expert", axis=0, tiled=True)
    ids = x[:, width : width + top].astype(jnp.int32)
    w = jnp.sum(
        jnp.where(ids == me, x[:, width + top : width + 2 * top].astype(jnp.float32), 0.0),
        axis=1,
        keepdims=True,
    )
    expert_load = (jnp.sum(w) / (tok_rows * top)).reshape(1)
    partial_value = local_partial(x, w, gate_weight[0], up_weight[0], bin_edges)
    paired = jnp.swapaxes(partial_value.reshape(-1, 2, replicas, share), 1, 2).reshape(
        -1, 2 * hidden_units
    )
    mine = lax.psum_scatter(paired, "replica", scatter_dimension=1, tiled=True).astype(jnp.float32)
    hidden_piece = (jax.nn.silu(mine[:, :share]) * mine[:, share:]).astype(jnp.bfloat16)
    hidden = lax.all_gather(hidden_piece, "replica", axis=1, tiled=True)
    result = jnp.dot(hidden, down_weight[0], preferred_element_type=jnp.float32)
    result = (w * result).astype(jnp.bfloat16)
    mixed = lax.psum_scatter(result, "expert", scatter_dimension=0, tiled=True)
    return (mixed, expert_load)


def solution(mesh):
    return jax.shard_map(
        body,
        mesh=mesh,
        in_specs=(
            P("expert", "replica"),
            P("expert", None),
            P("expert", None),
            P("expert", "replica", None),
            P("expert", "replica", None),
            P("expert", None, "replica"),
            P(),
        ),
        out_specs=(P("expert", "replica"), P("expert")),
        check_vma=False,
    )
```

```python
import functools

import jax
import jax.numpy as jnp
from jax import lax
from jax.experimental import pallas as pl
from jax.experimental.pallas import tpu as pltpu
from jax.sharding import PartitionSpec as P

FINE = 8
clip_parts = 8


def round_up(level):
    near = level.astype(jnp.bfloat16)
    wide = near.astype(jnp.float32)
    above = (wide * (1.0 + 0.75 * 2.0**-7)).astype(jnp.bfloat16)
    return jnp.where(wide < level, above.astype(jnp.float32), wide).astype(jnp.bfloat16)


def counts(magnitude_ref, level):
    rows, width = magnitude_ref.shape
    bound = jnp.broadcast_to(round_up(level), (16, width))
    one, zero = jnp.ones((16, width), jnp.bfloat16), jnp.zeros((16, width), jnp.bfloat16)

    def step(i, total):
        for k in range(8):
            block = magnitude_ref[pl.ds(pl.multiple_of(i * 128 + k * 16, 16), 16), :]
            total = total + jnp.where(block >= bound, one, zero)
        return total

    total = lax.fori_loop(0, rows // 128, step, zero)
    return jnp.sum(total.astype(jnp.float32), axis=0, keepdims=True)


def pick(index, values, other):
    result = jnp.full(index.shape, other, jnp.float32)
    for j, value in enumerate(values):
        result = jnp.where(index == j, value, result)
    return result


def clip_scale(magnitude_ref, edges, limit):
    width = magnitude_ref.shape[1]
    chosen = jnp.zeros((1, width), jnp.int32)
    step = 1
    while step * 2 < len(edges):
        step *= 2
    while step:
        passed = counts(magnitude_ref, pick(chosen + (step - 1), edges, edges[-1])) > limit
        chosen = jnp.where(passed, chosen + step, chosen)
        step //= 2
    upper = pick(chosen, edges, edges[-1])
    lower = pick(chosen - 1, edges, 0.0)
    picked = jnp.zeros((1, width), jnp.int32)

    def level(index):
        part = lower + (upper - lower) * ((index + 1).astype(jnp.float32) / FINE)
        return jnp.where(index >= FINE - 1, upper, part)

    step = FINE // 2
    while step:
        passed = counts(magnitude_ref, level(picked + (step - 1))) > limit
        picked = jnp.where(passed, picked + step, picked)
        step //= 2
    return level(picked)


def local_kernel(bins, edges_ref, x_ref, w_ref, gate_ref, up_ref, out_ref, magnitude, total):
    k = pl.program_id(0)
    named = w_ref[...] > 0.0
    limit = jnp.floor(jnp.sum(named.astype(jnp.float32)) / clip_parts)
    x = x_ref[...]
    magnitude[...] = jnp.where(named, jnp.abs(x.astype(jnp.float32)), 0.0).astype(jnp.bfloat16)
    edges = [edges_ref[j] for j in range(bins)]
    scale = clip_scale(magnitude, edges, limit).astype(jnp.bfloat16)
    x = jnp.minimum(jnp.maximum(x, -scale), scale)
    half = gate_ref.shape[1]

    @pl.when(k == 0)
    def _():
        total[...] = jnp.zeros_like(total)

    total[:, :half] += jnp.dot(x, gate_ref[...], preferred_element_type=jnp.float32)
    total[:, half:] += jnp.dot(x, up_ref[...], preferred_element_type=jnp.float32)

    @pl.when(k == pl.num_programs(0) - 1)
    def _():
        out_ref[...] = total[...].astype(out_ref.dtype)


def local_partial(x, w, gate, up, edges):
    rows, width = x.shape[0], gate.shape[0]
    hidden = gate.shape[1]
    chunk = 512 if width % 512 == 0 else 256
    return pl.pallas_call(
        functools.partial(local_kernel, edges.shape[0]),
        out_shape=jax.ShapeDtypeStruct((rows, 2 * hidden), jnp.bfloat16),
        grid=(width // chunk,),
        in_specs=[
            pl.BlockSpec(memory_space=pltpu.SMEM),
            pl.BlockSpec((rows, chunk), lambda k: (0, k)),
            pl.BlockSpec((rows, 1), lambda k: (0, 0)),
            pl.BlockSpec((chunk, hidden), lambda k: (k, 0)),
            pl.BlockSpec((chunk, hidden), lambda k: (k, 0)),
        ],
        out_specs=pl.BlockSpec((rows, 2 * hidden), lambda k: (0, 0)),
        scratch_shapes=[
            pltpu.VMEM((rows, chunk), jnp.bfloat16),
            pltpu.VMEM((rows, 2 * hidden), jnp.float32),
        ],
        compiler_params=pltpu.CompilerParams(vmem_limit_bytes=60 * 2**20),
    )(edges, x, w, gate, up)


MESH = pl.DeviceIdType.MESH
NOTE = 128
KC = 4
VMEM_MOST = 67043328


def fused_kernel(
    bins, top, x_hbm, gate_hbm, up_hbm, down_hbm, edges_ref, out_ref, load_ref,
    xg, mag, wv, gu, down, sbuf, rbuf, own, hid, outb, sibr, scw, rcw, sccw, rccw,
    load_sems, ring_send, ring_recv, sib_send, sib_recv, part_send, part_recv,
    hid_send, hid_recv, pair_send, pair_recv, cw_send, cw_recv, ccw_send, ccw_recv,
):
    experts = lax.axis_size("expert")
    me, r = lax.axis_index("expert"), lax.axis_index("replica")
    chips = experts // 2
    half_ring = chips // 2
    c = lax.rem(me, 2)
    chip = lax.div(me, 2)
    odd, low = lax.rem(chip, 2), lax.div(chip, 2)
    pos = (1 - odd) * low + odd * (chips - 1 - low)

    def at(place):
        place = lax.rem(place + chips, chips)
        back = lax.div(place, half_ring)
        number = (1 - back) * (2 * place) + back * (2 * (chips - 1 - place) + 1)
        return (number * 2 + c, r)

    right, left = at(pos + 1), at(pos - 1)
    sibling = (chip * 2 + (1 - c), r)
    partner = (me, 1 - r)

    rows, wide = xg.shape
    tok = rows // experts
    width = wide - NOTE
    share = hid.shape[1] // 2
    tile = own.shape[2]
    tiles = own.shape[0]
    blocks = half_ring
    brows = rows // blocks

    own_load = pltpu.make_async_copy(
        x_hbm, xg.at[pl.ds(pl.multiple_of((2 + c) * tok, tok), tok), :], load_sems.at[0]
    )
    own_load.start()
    weight_loads = [
        pltpu.make_async_copy(gate_hbm, gu.at[0], load_sems.at[1]),
        pltpu.make_async_copy(up_hbm, gu.at[1], load_sems.at[2]),
        pltpu.make_async_copy(down_hbm, down, load_sems.at[3]),
    ]
    for copy in weight_loads:
        copy.start()

    barrier = pltpu.get_barrier_semaphore()
    for other in (right, left, sibling, partner):
        pl.semaphore_signal(barrier, inc=1, device_id=other, device_id_type=MESH)
    pl.semaphore_wait(barrier, 4)
    own_load.wait()

    def slot(distance):
        if distance == 0:
            return 1
        if abs(distance) == half_ring:
            return 0
        return 2 * (half_ring - abs(distance)) + (0 if distance > 0 else 1)

    def block(s, core, k):
        step = width // KC
        begin, size = (0, NOTE + step) if k == 0 else (NOTE + k * step, step)
        start = pl.multiple_of((s * 2 + core) * tok, tok)
        return xg.at[pl.ds(start, tok), pl.ds(begin, size)]

    def ring_copy(distance, k, way):
        nearer = slot(distance)
        further = slot(distance + way)
        return pltpu.make_async_remote_copy(
            src_ref=block(nearer, c, k), dst_ref=block(further, c, k),
            send_sem=ring_send.at[k, 0 if way > 0 else 1, abs(distance)],
            recv_sem=ring_recv.at[k, further],
            device_id=right if way > 0 else left, device_id_type=MESH,
        )

    def sib_copy(s, k):
        return pltpu.make_async_remote_copy(
            src_ref=block(s, c, k), dst_ref=block(s, c, k),
            send_sem=sib_send.at[k, s], recv_sem=sib_recv.at[k, s],
            device_id=sibling, device_id_type=MESH,
        )

    def sib_arrival(s, k):
        return pltpu.make_async_remote_copy(
            src_ref=block(s, 1 - c, k), dst_ref=block(s, 1 - c, k),
            send_sem=sib_send.at[k, s], recv_sem=sib_recv.at[k, s],
            device_id=sibling, device_id_type=MESH,
        )

    started = []
    events = sorted((2 * h + k, k, h) for k in range(KC) for h in range(half_ring + 1))
    for _, k, h in events:
        for way in (1, -1):
            hops = half_ring if (way > 0) == (k % 2 == 0) else half_ring - 1
            if h > hops:
                continue
            if h > 0:
                ring_copy(way * (h - 1), k, way).wait_recv()
            if h < hops:
                copy = ring_copy(way * h, k, way)
                copy.start()
                started.append(copy)
            if h > 0 or way > 0:
                copy = sib_copy(slot(way * h), k)
                copy.start()
                started.append(copy)
    for k in range(KC):
        for s in range(chips):
            sib_arrival(s, k).wait_recv()
    for copy in started:
        copy.wait_send()

    lane = lax.broadcasted_iota(jnp.int32, (rows, NOTE), 1)
    wv[...] = jnp.sum(
        jnp.where(lane == me, xg[:, 0:NOTE].astype(jnp.float32), 0.0), axis=1, keepdims=True
    )
    load_ref[...] = jnp.full(load_ref.shape, jnp.sum(wv[...]) / (tok * top), jnp.float32)
    limit = jnp.floor(jnp.sum((wv[...] > 0.0).astype(jnp.float32)) / clip_parts)
    edges = [edges_ref[j] for j in range(bins)]
    chunk = mag.shape[1]

    def clip_step(k, carry):
        columns = pl.ds(pl.multiple_of(NOTE + k * chunk, 128), chunk)
        x = xg[:, columns]
        mag[...] = jnp.where(wv[...] > 0.0, jnp.abs(x.astype(jnp.float32)), 0.0).astype(jnp.bfloat16)
        scale = clip_scale(mag, edges, limit).astype(jnp.bfloat16)
        xg[:, columns] = jnp.minimum(jnp.maximum(xg[:, columns], -scale), scale)
        return carry

    lax.fori_loop(0, width // chunk, clip_step, 0)

    weight_loads[0].wait()
    weight_loads[1].wait()
    per = tiles // 2

    def product(j, side, span):
        begin = pl.multiple_of(side * share + lax.rem(j, per) * tile, 128)
        return jnp.dot(
            xg[span, NOTE:], gu[lax.div(j, per), :, pl.ds(begin, tile)],
            preferred_element_type=jnp.float32,
        )

    def part_copy(j, i):
        span = pl.ds(pl.multiple_of(i * brows, brows), brows)
        return pltpu.make_async_remote_copy(
            src_ref=sbuf.at[j, span, :], dst_ref=rbuf.at[j, span, :],
            send_sem=part_send.at[j, i], recv_sem=part_recv.at[j, i],
            device_id=partner, device_id_type=MESH,
        )

    def hid_copy(i, side):
        place = hid.at[
            pl.ds(pl.multiple_of(i * brows, brows), brows),
            pl.ds(pl.multiple_of(side * share, 128), share),
        ]
        return pltpu.make_async_remote_copy(
            src_ref=place, dst_ref=place, send_sem=hid_send.at[i], recv_sem=hid_recv.at[i],
            device_id=partner, device_id_type=MESH,
        )

    middle = width // 2

    def pair_copy(s):
        span = pl.ds(pl.multiple_of((s * 2 + (1 - c)) * tok, tok), tok)
        return pltpu.make_async_remote_copy(
            src_ref=outb.at[span, :], dst_ref=sibr.at[s],
            send_sem=pair_send.at[s], recv_sem=pair_recv.at[s],
            device_id=sibling, device_id_type=MESH,
        )

    def sum_copy(sent, came, send_sem, recv_sem, s, first, target):
        cols = pl.ds(first, middle) if s == 0 else pl.ds(0, width)
        return pltpu.make_async_remote_copy(
            src_ref=sent.at[s, :, cols], dst_ref=came.at[s, :, cols],
            send_sem=send_sem.at[s], recv_sem=recv_sem.at[s],
            device_id=target, device_id_type=MESH,
        )

    def cw_copy(s):
        return sum_copy(scw, rcw, cw_send, cw_recv, s, 0, right)

    def ccw_copy(s):
        return sum_copy(sccw, rccw, ccw_send, ccw_recv, s, middle, left)

    def share_of(s, begin, size):
        span = pl.ds(pl.multiple_of((s * 2 + c) * tok, tok), tok)
        mine = outb[span, begin : begin + size].astype(jnp.float32)
        return mine + sibr[s, :, begin : begin + size].astype(jnp.float32)

    def stage_send(i):
        span = pl.ds(i * brows, brows)

        def step(j, carry):
            sbuf[j, span, :] = product(j, 1 - r, span).astype(jnp.bfloat16)
            part_copy(j, i).start()
            return carry

        lax.fori_loop(0, tiles, step, 0)

    def stage_hidden(i):
        span = pl.ds(i * brows, brows)

        def step(j, carry):
            own[j, span, :] = product(j, r, span)
            return carry

        lax.fori_loop(0, tiles, step, 0)
        for j in range(tiles):
            part_copy(j, i).wait_recv()
        for j in range(per):
            gate = own[j, span, :] + rbuf[j, span, :].astype(jnp.float32)
            up = own[j + per, span, :] + rbuf[j + per, span, :].astype(jnp.float32)
            place = pl.ds(pl.multiple_of(r * share + j * tile, 128), tile)
            hid[span, place] = (gate / (1.0 + jnp.exp(-gate)) * up).astype(jnp.bfloat16)
        hid_copy(i, r).start()

    piece = 512 if width % 512 == 0 else 128

    def stage_down(i):
        span = pl.ds(i * brows, brows)
        hid_copy(i, 1 - r).wait_recv()
        if i == 0:
            weight_loads[2].wait()

        def step(n, carry):
            columns = pl.ds(pl.multiple_of(n * piece, 128), piece)
            result = jnp.dot(hid[span, :], down[:, columns], preferred_element_type=jnp.float32)
            outb[span, columns] = (wv[span, :] * result).astype(jnp.bfloat16)
            return carry

        lax.fori_loop(0, width // piece, step, 0)
        pair_copy(2 * i).start()
        pair_copy(2 * i + 1).start()
        pair_copy(2 * i).wait_recv()
        pair_copy(2 * i + 1).wait_recv()
        for sums, came, copy, s, first in (
            (scw, rcw, cw_copy, 2 * i + 1 if i else 0, 0),
            (sccw, rccw, ccw_copy, 2 * i, middle),
        ):
            if i:
                copy(i - 1).wait_recv()
            for begin in (0, middle):
                cols = slice(begin, begin + middle)
                if i == 0 and begin != first:
                    continue
                value = share_of(s, begin, middle)
                if i > 1 or (i == 1 and begin == first):
                    value = value + came[i - 1, :, cols].astype(jnp.float32)
                sums[i, :, cols] = value.astype(jnp.bfloat16)
            copy(i).start()

    for t in range(blocks + 2):
        if t < blocks:
            stage_send(t)
        if 1 <= t <= blocks:
            stage_hidden(t - 1)
        if t >= 2:
            stage_down(t - 2)
    last = blocks - 1
    cw_copy(last).wait_recv()
    ccw_copy(last).wait_recv()
    for begin in (0, middle):
        cols = slice(begin, begin + middle)
        value = share_of(1, begin, middle) + rcw[last, :, cols].astype(jnp.float32)
        out_ref[:, cols] = (value + rccw[last, :, cols].astype(jnp.float32)).astype(out_ref.dtype)
    for i in range(blocks):
        for j in range(tiles):
            part_copy(j, i).wait_send()
        hid_copy(i, r).wait_send()
        cw_copy(i).wait_send()
        ccw_copy(i).wait_send()
    for s in range(chips):
        pair_copy(s).wait_send()


def fused_scratch(experts, tok, width, hidden):
    rows, chips = experts * tok, experts // 2
    share = hidden // 2
    tile = 256 if share % 256 == 0 else 128
    tiles = 2 * share // tile
    chunk = 512 if width % 512 == 0 else 128
    bf, f32 = jnp.bfloat16, jnp.float32
    ring = (chips // 2, tok, width)
    return [
        ((rows, NOTE + width), bf), ((rows, chunk), bf), ((rows, 1), f32),
        ((2, width, hidden), bf), ((hidden, width), bf),
        ((tiles, rows, tile), bf), ((tiles, rows, tile), bf), ((tiles, rows, tile), f32),
        ((rows, hidden), bf), ((rows, width), bf), ((chips, tok, width), bf),
        (ring, bf), (ring, bf), (ring, bf), (ring, bf),
    ]


def fused_fits(experts, replicas, tok, width, hidden):
    held = 0
    for shape, dtype in fused_scratch(experts, tok, width, hidden):
        size = jnp.dtype(dtype).itemsize
        for n in shape[:-1] + (max(shape[-1], 128),):
            size *= n
        held += size
    even = experts % 4 == 0 and replicas == 2 and tok % 16 == 0 and experts <= NOTE
    return even and width % (KC * 128) == 0 and held < 0.9 * VMEM_MOST


def fused(x, gate, up, down, edges, experts, top):
    tok, wide = x.shape
    width, hidden = gate.shape
    chips = experts // 2
    shapes = fused_scratch(experts, tok, width, hidden)
    tiles, blocks = shapes[5][0][0], chips // 2
    dma = pltpu.SemaphoreType.DMA
    any_spec = pl.BlockSpec(memory_space=pl.ANY)
    vmem = pl.BlockSpec(memory_space=pltpu.VMEM)
    return pl.pallas_call(
        functools.partial(fused_kernel, edges.shape[0], top),
        out_shape=(
            jax.ShapeDtypeStruct((tok, width), jnp.bfloat16),
            jax.ShapeDtypeStruct((1, 128), jnp.float32),
        ),
        in_specs=[any_spec] * 4 + [pl.BlockSpec(memory_space=pltpu.SMEM)],
        out_specs=(vmem, vmem),
        scratch_shapes=[pltpu.VMEM(shape, dtype) for shape, dtype in shapes]
        + [
            dma((4,)), dma((KC, 2, blocks)), dma((KC, chips)), dma((KC, chips)), dma((KC, chips)),
            dma((tiles, blocks)), dma((tiles, blocks)), dma((blocks,)), dma((blocks,)),
            dma((chips,)), dma((chips,)), dma((blocks,)), dma((blocks,)),
            dma((blocks,)), dma((blocks,)),
        ],
        compiler_params=pltpu.CompilerParams(
            collective_id=0, has_side_effects=True, vmem_limit_bytes=VMEM_MOST
        ),
    )(x, gate, up, down, edges)


def body(tokens, expert_ids, route_weights, gate_weight, up_weight, down_weight, bin_edges):
    experts = lax.axis_size("expert")
    me = lax.axis_index("expert")
    replicas = lax.axis_size("replica")
    tok_rows, width = tokens.shape
    top = expert_ids.shape[1]
    hidden_units = gate_weight.shape[2]
    share = hidden_units // replicas
    if fused_fits(experts, replicas, tok_rows, width, hidden_units):
        numbers = jnp.arange(NOTE, dtype=jnp.int32)
        notes = sum(
            jnp.where(expert_ids[:, k : k + 1] == numbers, route_weights[:, k : k + 1], 0)
            for k in range(top)
        )
        mixed, load = fused(
            jnp.concatenate([notes.astype(jnp.bfloat16), tokens], axis=1),
            gate_weight[0], up_weight[0], down_weight[0], bin_edges, experts, top,
        )
        return mixed, load[0, :1]
    notes = jnp.concatenate([expert_ids.astype(jnp.bfloat16), route_weights], axis=1)
    notes = jnp.pad(notes, ((0, 0), (0, 128 - 2 * top)))
    x = lax.all_gather(jnp.concatenate([tokens, notes], axis=1), "expert", axis=0, tiled=True)
    ids = x[:, width : width + top].astype(jnp.int32)
    w = jnp.sum(
        jnp.where(ids == me, x[:, width + top : width + 2 * top].astype(jnp.float32), 0.0),
        axis=1,
        keepdims=True,
    )
    expert_load = (jnp.sum(w) / (tok_rows * top)).reshape(1)
    partial_value = local_partial(x, w, gate_weight[0], up_weight[0], bin_edges)
    paired = jnp.swapaxes(partial_value.reshape(-1, 2, replicas, share), 1, 2).reshape(
        -1, 2 * hidden_units
    )
    mine = lax.psum_scatter(paired, "replica", scatter_dimension=1, tiled=True).astype(jnp.float32)
    hidden_piece = (jax.nn.silu(mine[:, :share]) * mine[:, share:]).astype(jnp.bfloat16)
    hidden = lax.all_gather(hidden_piece, "replica", axis=1, tiled=True)
    result = jnp.dot(hidden, down_weight[0], preferred_element_type=jnp.float32)
    result = (w * result).astype(jnp.bfloat16)
    mixed = lax.psum_scatter(result, "expert", scatter_dimension=0, tiled=True)
    return (mixed, expert_load)


def solution(mesh):
    return jax.shard_map(
        body,
        mesh=mesh,
        in_specs=(
            P("expert", "replica"),
            P("expert", None),
            P("expert", None),
            P("expert", "replica", None),
            P("expert", "replica", None),
            P("expert", None, "replica"),
            P(),
        ),
        out_specs=(P("expert", "replica"), P("expert")),
        check_vma=False,
    )
```
